32 devices in a mesh: dp: 8 (over y, x, core), tensor: 4 (over z).
Axes of the slice: x: 2, y: 2, z: 4, core: 2. Of those that a mesh axis runs over, the one named last changes fastest.
Arguments:
- inputs: bfloat16 [64, 256, 1152], P('dp'), may hold values from -6 to 6
- cotangent: bfloat16 [64, 256, 1152], P('dp'), may hold values from -6 to 6
- counts: int32 [8], P('dp'), may hold values from 1 to 8, as said below
- time_ids: int32 [64], P('dp'), may hold values from 0 to 999
- class_ids: int32 [64], P('dp'), may hold values from 0 to 1000
- time_table: bfloat16 [1000, 1152], replicated, may hold values from -4 to 4
- class_table: bfloat16 [1001, 1152], replicated, may hold values from -4 to 4
- ada_weight: bfloat16 [1152, 6, 1152], P(None, None, 'tensor'), may hold values from -0.1875 to 0.1875
- ada_bias: bfloat16 [6, 1152], P(None, 'tensor'), may hold values from -1.75 to 1.75
- qkv_weight: bfloat16 [1152, 3, 1152], P(None, None, 'tensor'), may hold values from -0.1875 to 0.1875
- qv_bias: bfloat16 [2, 1152], P(None, 'tensor'), may hold values from -1.75 to 1.75
- proj_weight: bfloat16 [1152, 1152], P('tensor'), may hold values from -1.5 to 1.5
- proj_bias: bfloat16 [1152], replicated, may hold values from -1.75 to 1.75
- up_weight: bfloat16 [1152, 4608], P(None, 'tensor'), may hold values from -0.1875 to 0.1875
- up_bias: bfloat16 [4608], P('tensor'), may hold values from -1.75 to 1.75
- down_weight: bfloat16 [4608, 1152], P('tensor'), may hold values from -0.09375 to 0.09375
- down_bias: bfloat16 [1152], replicated, may hold values from -1.75 to 1.75
Outputs:
- outputs: bfloat16 [64, 256, 1152], P('dp')
- grad_inputs: bfloat16 [64, 256, 1152], P('dp')
- grad_time_table: float32 [1000, 1152], replicated
- grad_class_table: float32 [1001, 1152], replicated
- grad_ada_weight: float32 [1152, 6, 1152], P(None, None, 'tensor')
- grad_ada_bias: float32 [6, 1152], P(None, 'tensor')
- grad_qkv_weight: float32 [1152, 3, 1152], P(None, None, 'tensor')
- grad_qv_bias: float32 [2, 1152], P(None, 'tensor')
- grad_proj_weight: float32 [1152, 1152], P('tensor')
- grad_proj_bias: float32 [1152], replicated
- grad_up_weight: float32 [1152, 4608], P(None, 'tensor')
- grad_up_bias: float32 [4608], P('tensor')
- grad_down_weight: float32 [4608, 1152], P('tensor')
- grad_down_bias: float32 [1152], replicated
The draws below stay inside these ranges and needn't reach their ends.
Inputs may be any that keep to these rules, and one draw needn't show every extreme that they name: Each index of dp holds 8 image slots whose first counts live; at least one index has all 8 live.
All inputs are finite; a program needn't handle non-finite values.
Results may differ from the reference program's by a relative error of at most 0.014.
The reference program's roundings to bfloat16 on the way count: a program that leaves them out, or rounds other values in their place, can miss the bound.
Values sent between devices are 32-bit elements; how exact they have to be, the bound alone decides.
No kernel may reach another device: no remote copies, remote signals or barrier semaphores. Data moves between devices by JAX's collectives and lax.ppermute only.
A program may use at most 256 MiB of HBM per device.

```python
import jax
import jax.numpy as jnp
from jax import lax

D = 1152
HEADS = 16
HEAD_DIM = 72
FF = 4608
SEQ = 256
CLASSES = 1001
TSTEPS = 1000
IMG_CAP = 8
IMAGES = 64
N_DP = 8


def draw_counts(key, part):
    first_key, second_key = jax.random.split(key)
    drawn = jax.random.randint(first_key, (N_DP,), 1, IMG_CAP + 1)
    chosen = jax.random.randint(second_key, (), 0, N_DP)
    return jnp.where(jnp.arange(N_DP) == chosen, IMG_CAP, drawn).astype(jnp.int32)


def touch_ends(values, own_key, low, high):
    index_at = [jax.random.randint(jax.random.fold_in(own_key, axis), (), 0, length) for axis, length in enumerate(values.shape)]
    widest = values.shape.index(max(values.shape))
    beside = index_at[:widest] + [(index_at[widest] + 1) % values.shape[widest]] + index_at[widest + 1:]
    return values.at[tuple(index_at)].set(low).at[tuple(beside)].set(high)


def shard_levels(rng, extent, cuts, least, top_value):
    factor_of, own = 1.0, jax.random.fold_in(rng, 6)
    for dim, shards_of in cuts:
        steps = jnp.exp(jax.random.uniform(jax.random.fold_in(own, dim), (shards_of,), jnp.float32, least / len(cuts), top_value / len(cuts)))
        factor_of = factor_of * jnp.repeat(steps, extent[dim] // shards_of).reshape([-1 if axis == dim else 1 for axis in range(len(extent))])
    return factor_of


def noise(stream_key, shape, scale, limit, pieces=(), held_as=jnp.bfloat16):
    values = jax.random.normal(stream_key, shape, jnp.float32) * scale
    if len(pieces) > 0:
        values = shard_levels(stream_key, shape, pieces, -0.22, 0.18) * values
    return jnp.clip(values, min=-limit, max=limit).astype(held_as)


def setup_inputs(seed: int = 0) -> dict:
    splits = jax.random.split(jax.random.key(seed), 18)
    return {
        "inputs": noise(splits[0], (IMAGES, SEQ, D), 1.0, 6.0, ((0, 8),)),
        "cotangent": noise(splits[1], (IMAGES, SEQ, D), 1.0, 6.0, ((0, 8),)),
        "counts": draw_counts(jax.random.fold_in(splits[17], 71), 0),
        "time_ids": touch_ends(jax.random.randint(splits[3], (IMAGES,), 0, TSTEPS), jax.random.fold_in(splits[3], 1), 0, TSTEPS - 1).astype(jnp.int32),
        "class_ids": touch_ends(jax.random.randint(splits[4], (IMAGES,), 0, CLASSES), jax.random.fold_in(splits[4], 1), 0, CLASSES - 1).astype(jnp.int32),
        "time_table": noise(splits[5], (TSTEPS, D), 0.7, 4.0),
        "class_table": noise(splits[6], (CLASSES, D), 0.7, 4.0),
        "ada_weight": noise(splits[7], (D, 6, D), D ** -0.5, 0.1875, ((2, 4),)),
        "ada_bias": noise(splits[8], (6, D), 0.3, 1.75, ((1, 4),)),
        "qkv_weight": noise(splits[9], (D, 3, D), D ** -0.5, 0.1875, ((2, 4),)),
        "qv_bias": noise(splits[10], (2, D), 0.3, 1.75, ((1, 4),)),
        "proj_weight": noise(splits[11], (D, D), (max(D // 64, 1)) ** -0.5, 1.5, ((0, 4),)),
        "proj_bias": noise(splits[12], (D,), 0.3, 1.75),
        "up_weight": noise(splits[13], (D, FF), D ** -0.5, 0.1875, ((1, 4),)),
        "up_bias": noise(splits[14], (FF,), 0.3, 1.75, ((0, 4),)),
        "down_weight": noise(splits[15], (FF, D), FF ** -0.5, 0.09375, ((0, 4),)),
        "down_bias": noise(splits[16], (D,), 0.3, 1.75),
    }


EPSILON = 1e-06
GELU_ROOT = 0.7978845608028654
GELU_CUBIC = 0.044715

@jax.custom_vjp
def low(v):
    return lax.optimization_barrier(v.astype(jnp.bfloat16)).astype(jnp.float32)

@jax.custom_vjp
def low_back(v):
    return v

def low_keep(v):
    return (low(v), None)

def low_pass(kept, grad):
    return (grad,)

def back_keep(v):
    return (v, None)

def back_low(kept, grad):
    return (low(grad),)
low.defvjp(low_keep, low_pass)
low_back.defvjp(back_keep, back_low)

def rounded_both(values):
    return low_back(low(values))

def layer_norm(values):
    average = lax.optimization_barrier(jnp.mean(values, axis=-1, keepdims=True))
    centred = values - average
    spread = lax.optimization_barrier(jnp.mean(centred * centred, axis=-1, keepdims=True))
    return centred * lax.rsqrt(spread + EPSILON)

def gelu_tanh(values):
    return 0.5 * values * (1.0 + jnp.tanh(GELU_ROOT * (values + GELU_CUBIC * values * values * values)))

def forward(params, inputs, time_pick, class_pick, live):
    time_table, class_table, ada_weight, ada_bias, qkv_weight, qv_bias, proj_weight, proj_bias, up_weight, up_bias, down_weight, down_bias = params
    highest = lax.Precision.HIGHEST
    groups = inputs.shape[0]
    condition = jnp.dot(time_pick, time_table, precision=highest) + jnp.dot(class_pick, class_table, precision=highest)
    silu_cond = low(jax.nn.silu(condition))
    modulation = low_back(jnp.einsum('gd,dke->gke', silu_cond, ada_weight, precision=highest) + ada_bias)
    shift_attn = modulation[:, 0][:, None, :]
    scale_attn = modulation[:, 1][:, None, :]
    gate_attn = modulation[:, 2][:, None, :]
    shift_mlp = modulation[:, 3][:, None, :]
    scale_mlp = modulation[:, 4][:, None, :]
    gate_mlp = modulation[:, 5][:, None, :]
    hidden_attn = low(layer_norm(inputs) * (1.0 + scale_attn) + shift_attn)
    projected = jnp.einsum('gsd,dke->gske', hidden_attn, qkv_weight, precision=highest)
    shape_heads = (groups, SEQ, HEADS, HEAD_DIM)
    query_heads = rounded_both(projected[:, :, 0] + qv_bias[0]).reshape(shape_heads)
    key_heads = rounded_both(projected[:, :, 1]).reshape(shape_heads)
    value_heads = rounded_both(projected[:, :, 2] + qv_bias[1]).reshape(shape_heads)
    scores = low_back(jnp.einsum('gqhe,gkhe->ghqk', query_heads, key_heads, precision=highest) * HEAD_DIM ** (-0.5))
    soft_probs = low(jax.nn.softmax(scores, axis=-1))
    heads_out = rounded_both(jnp.einsum('ghqk,gkhe->gqhe', soft_probs, value_heads, precision=highest).reshape(groups, SEQ, D))
    attention = low_back(jnp.einsum('gse,ed->gsd', heads_out, proj_weight, precision=highest) + proj_bias)
    middle = inputs + gate_attn * attention
    hidden_mlp = low(layer_norm(middle) * (1.0 + scale_mlp) + shift_mlp)
    pre_act = low_back(jnp.einsum('gsd,df->gsf', hidden_mlp, up_weight, precision=highest) + up_bias)
    activated = low(gelu_tanh(pre_act))
    branch = low_back(jnp.einsum('gsf,fd->gsd', activated, down_weight, precision=highest) + down_bias)
    return (middle + gate_mlp * branch) * live[:, None, None]

def reference(inputs, cotangent, counts, time_ids, class_ids, time_table, class_table, ada_weight, ada_bias, qkv_weight, qv_bias, proj_weight, proj_bias, up_weight, up_bias, down_weight, down_bias):
    params = tuple((member.astype(jnp.float32) for member in (time_table, class_table, ada_weight, ada_bias, qkv_weight, qv_bias, proj_weight, proj_bias, up_weight, up_bias, down_weight, down_bias)))
    slot_index = jnp.arange(IMG_CAP, dtype=jnp.int32)
    live_all = (slot_index[None, :] < counts[:, None]).astype(jnp.float32)
    grouped = (inputs.reshape(N_DP, IMG_CAP, SEQ, D), cotangent.reshape(N_DP, IMG_CAP, SEQ, D), time_ids.reshape(N_DP, IMG_CAP), class_ids.reshape(N_DP, IMG_CAP), live_all)
    time_levels = jnp.arange(TSTEPS, dtype=jnp.int32)
    class_levels = jnp.arange(CLASSES, dtype=jnp.int32)

    def group_step(totals, member):
        block_in, block_cot, block_time, block_class, block_live = member
        time_pick = (block_time[:, None] == time_levels[None, :]).astype(jnp.float32)
        class_pick = (block_class[:, None] == class_levels[None, :]).astype(jnp.float32)

        def forward_group(weights_all, values):
            return forward(weights_all, values, time_pick, class_pick, block_live)
        result, pullback = jax.vjp(forward_group, params, block_in.astype(jnp.float32))
        grad_params, grad_block = pullback(block_cot.astype(jnp.float32))
        totals = jax.tree.map(jnp.add, totals, grad_params)
        return (totals, (result.astype(jnp.bfloat16), grad_block.astype(jnp.bfloat16)))
    zero_grads = tuple((jnp.zeros_like(member) for member in params))
    gradients, (results, grad_blocks) = lax.scan(group_step, zero_grads, grouped)
    return (results.reshape(N_DP * IMG_CAP, SEQ, D), grad_blocks.reshape(N_DP * IMG_CAP, SEQ, D), gradients[0], gradients[1], gradients[2], gradients[3], gradients[4], gradients[5], gradients[6], gradients[7], gradients[8], gradients[9], gradients[10], gradients[11])
```

```python
import functools

import jax
import jax.numpy as jnp
from jax import lax
from jax.experimental import pallas as pl
from jax.experimental.pallas import tpu as pltpu
from jax.sharding import PartitionSpec as P

HEAD_DIM = 72
EPSILON = 1e-06
GELU_ROOT = 0.7978845608028654
GELU_CUBIC = 0.044715
WIDE = jnp.float32
NARROW = jnp.bfloat16


def norm_parts(values):
    average = jnp.mean(values, axis=-1, keepdims=True)
    centred = values - average
    spread = jnp.mean(centred * centred, axis=-1, keepdims=True)
    inverse = lax.rsqrt(spread + EPSILON)
    return (centred * inverse, inverse)


def norm_back(upstream, normed, inverse):
    first_mean = jnp.mean(upstream, axis=-1, keepdims=True)
    second_mean = jnp.mean(upstream * normed, axis=-1, keepdims=True)
    return inverse * (upstream - first_mean - normed * second_mean)


def gelu_parts(values):
    argument = GELU_ROOT * (values + GELU_CUBIC * values * values * values)
    tangent = jnp.tanh(argument)
    result = 0.5 * values * (1.0 + tangent)
    derivative = 0.5 * (1.0 + tangent) + 0.5 * values * (1.0 - tangent * tangent) * GELU_ROOT * (
        1.0 + 3.0 * GELU_CUBIC * values * values
    )
    return (result, derivative)


def ring(values, count, step):
    return lax.ppermute(values, "tensor", [(i, (i + step) % count) for i in range(count)])


def swap(values, count, bit):
    return lax.ppermute(values, "dp", [(i, i ^ bit) for i in range(count)])


def gather_small(values, count):
    slots = {0: values}
    half = count // 2
    for k in range(1, half + 1):
        slots[k] = ring(slots[k - 1], count, 1)
    for k in range(1, count - half):
        slots[count - k] = ring(slots[(count - k + 1) % count], count, -1)
    ascending = jnp.stack([slots[k] for k in range(count - 1, -1, -1)] * 2)
    start = count - 1 - lax.axis_index("tensor")
    return lax.dynamic_slice_in_dim(ascending, start, count, 0)


def gather_foreign(halves, tensor_count, dp_count, shared):
    half = tensor_count // 2
    slots = {0: tuple(halves)}
    for k in range(1, half):
        slots[k] = tuple(ring(part, tensor_count, 1) for part in slots[k - 1])
        slots[tensor_count - k] = tuple(
            ring(part, tensor_count, -1) for part in slots[(tensor_count - k + 1) % tensor_count]
        )
    slots[half] = (
        ring(slots[half - 1][0], tensor_count, 1),
        ring(slots[(half + 1) % tensor_count][1], tensor_count, -1),
    )
    order = [k for k in range(1, tensor_count) if k != half] + [half]
    mine = [slots[k] for k in order]
    if not shared:
        return mine
    across = [(swap(top, dp_count, 2), swap(bottom, dp_count, 4)) for top, bottom in mine]
    both = mine + across
    other_core = [tuple(swap(part, dp_count, 1) for part in pair) for pair in both]
    return both + other_core


NT = (((1,), (1,)), ((), ()))
NN = (((1,), (0,)), ((), ()))


def dot(left, right, dims):
    return lax.dot_general(left, right, dims, preferred_element_type=WIDE)


def mlp_kernel(
    live_ref,
    inputs_ref,
    attention_ref,
    cotangent_ref,
    modulation_ref,
    up_ref,
    up_bias_ref,
    down_ref,
    down_bias_ref,
    outputs_ref,
    d_middle_ref,
    d_attention_ref,
    hidden_ref,
    d_branch_ref,
    activated_ref,
    d_pre_ref,
    sums_ref,
    branch_ref,
    d_hidden_ref,
    *,
    chunks,
    size,
):
    live = jnp.where(pl.program_id(0) < live_ref[0], 1.0, 0.0)
    row = lambda index: modulation_ref[0, index : index + 1, :]
    gate_attn, shift_mlp, scale_mlp, gate_mlp = row(2), row(3), row(4), row(5)
    middle = inputs_ref[0].astype(WIDE) + gate_attn * attention_ref[0]
    normed, inverse = norm_parts(middle)
    hidden_ref[0] = (normed * (1.0 + scale_mlp) + shift_mlp).astype(NARROW)
    grad_out = cotangent_ref[0].astype(WIDE) * live
    d_branch_ref[0] = (gate_mlp * grad_out).astype(NARROW)
    branch_ref[...] = jnp.zeros_like(branch_ref)
    d_hidden_ref[...] = jnp.zeros_like(d_hidden_ref)
    sums_ref[0] = jnp.zeros_like(sums_ref[0])

    def chunk_step(chunk, carry):
        rows = pl.ds(pl.multiple_of(chunk * size, size), size)
        pre_act = dot(hidden_ref[0], up_ref[rows, :], NT) + up_bias_ref[pl.ds(chunk, 1), :]
        d_activated = dot(d_branch_ref[0], down_ref[rows, :], NT)
        value, slope = gelu_parts(pre_act)
        activated = value.astype(NARROW)
        d_pre = (d_activated * slope).astype(NARROW)
        branch_ref[...] += dot(activated, down_ref[rows, :], NN)
        d_hidden_ref[...] += dot(d_pre, up_ref[rows, :], NN)

        @pl.when(chunk == 0)
        def _():
            activated_ref[0] = activated
            d_pre_ref[0] = d_pre
            sums_ref[0, 6:7, :size] = jnp.sum(d_pre.astype(WIDE), axis=0, keepdims=True)

        return carry

    lax.fori_loop(0, chunks, chunk_step, 0)

    total = lambda values: jnp.sum(values, axis=0, keepdims=True)
    branch = branch_ref[...] + down_bias_ref[...]
    attention = attention_ref[0]
    middle = inputs_ref[0].astype(WIDE) + gate_attn * attention
    grad_out = cotangent_ref[0].astype(WIDE) * live
    outputs_ref[0] = ((middle + gate_mlp * branch) * live).astype(NARROW)
    sums_ref[0, 3:4, :] = total(grad_out * branch)
    sums_ref[0, 4:5, :] = total(d_branch_ref[0].astype(WIDE))
    normed, inverse = norm_parts(middle)
    d_hidden = d_hidden_ref[...]
    sums_ref[0, 1:2, :] = total(d_hidden)
    sums_ref[0, 2:3, :] = total(d_hidden * normed)
    d_middle = grad_out + norm_back(d_hidden * (1.0 + scale_mlp), normed, inverse)
    d_middle_ref[0] = d_middle
    sums_ref[0, 0:1, :] = total(d_middle * attention)
    d_attention = (gate_attn * d_middle).astype(NARROW)
    d_attention_ref[0] = d_attention
    sums_ref[0, 5:6, :] = total(d_attention.astype(WIDE))


def mlp_pass(counts, inputs, attention, cotangent, modulation, up, up_bias, down, down_bias, size):
    images, length, width = inputs.shape
    chunks = up.shape[0] // size
    tile = pl.BlockSpec((1, length, width), lambda g, live: (g, 0, 0))
    own_tile = pl.BlockSpec((1, length, size), lambda g, live: (g, 0, 0))
    whole = lambda array: pl.BlockSpec(
        array.shape, lambda g, live: (0, 0), pipeline_mode=pl.Buffered(1)
    )
    small = lambda rows: pl.BlockSpec((1, rows, width), lambda g, live: (g, 0, 0))
    token = lambda last, dtype: jax.ShapeDtypeStruct((images, length, last), dtype)
    return pl.pallas_call(
        functools.partial(mlp_kernel, chunks=chunks, size=size),
        grid_spec=pltpu.PrefetchScalarGridSpec(
            num_scalar_prefetch=1,
            grid=(images,),
            in_specs=[
                tile,
                tile,
                tile,
                small(6),
                whole(up),
                whole(up_bias),
                whole(down),
                whole(down_bias),
            ],
            out_specs=[tile, tile, tile, tile, tile, own_tile, own_tile, small(8)],
            scratch_shapes=[pltpu.VMEM((length, width), WIDE)] * 2,
        ),
        out_shape=[
            token(width, NARROW),
            token(width, WIDE),
            token(width, NARROW),
            token(width, NARROW),
            token(width, NARROW),
            token(size, NARROW),
            token(size, NARROW),
            jax.ShapeDtypeStruct((images, 8, width), WIDE),
        ],
        compiler_params=pltpu.CompilerParams(vmem_limit_bytes=60 * 1024 * 1024),
        cost_estimate=pl.CostEstimate(
            flops=8 * images * length * width * up.shape[0],
            bytes_accessed=images * length * width * 24 + 4 * up.shape[0] * width,
            transcendentals=images * length * up.shape[0],
        ),
        name="mlp_pass",
    )(counts, inputs, attention, cotangent, modulation, up, up_bias, down, down_bias)


def local(
    inputs,
    cotangent,
    counts,
    time_ids,
    class_ids,
    time_table,
    class_table,
    ada_weight,
    ada_bias,
    qkv_weight,
    qv_bias,
    proj_weight,
    proj_bias,
    up_weight,
    up_bias,
    down_weight,
    down_bias,
    *,
    tensor_count,
    dp_count,
):
    images, length, width = inputs.shape
    local_width = qkv_weight.shape[2]
    local_hidden = up_weight.shape[1]
    heads_here = local_width // HEAD_DIM
    heads = heads_here * tensor_count
    scaling = HEAD_DIM ** (-0.5)

    pieces = 4 if heads_here % 4 == 0 and dp_count % 8 == 0 else 1
    heads_piece = heads_here // pieces
    row_piece = heads_piece * HEAD_DIM
    hidden_piece = local_hidden // pieces
    index = lax.axis_index("dp")
    piece = (((index >> 1) ^ (index >> 2)) & 1) * 2 + (index & 1) if pieces == 4 else 0
    cut = lambda array, axis, size: (
        lax.dynamic_slice_in_dim(array, piece * size, size, axis) if pieces > 1 else array
    )
    qkv_rows = cut(qkv_weight, 2, row_piece).transpose(1, 2, 0).reshape(3 * row_piece, width)
    pad_row = lambda vector: jnp.pad(vector, (0, width - vector.shape[0]))[None, :]
    attn_bias_row = jnp.pad(
        pad_row(cut(qv_bias, 1, row_piece).reshape(2 * row_piece)), ((0, 7), (0, 0))
    )
    up_bias_row = jnp.pad(pad_row(cut(up_bias, 0, hidden_piece)), ((0, 7), (0, 0)))
    attn_halves = (
        jnp.concatenate([qkv_rows[: 2 * row_piece], attn_bias_row], 0).astype(WIDE),
        jnp.concatenate([qkv_rows[2 * row_piece :], cut(proj_weight, 0, row_piece)], 0).astype(WIDE),
    )
    mlp_halves = (
        jnp.concatenate([cut(up_weight, 1, hidden_piece).transpose(1, 0), up_bias_row], 0).astype(WIDE),
        cut(down_weight, 0, hidden_piece).astype(WIDE),
    )

    condition = (
        jnp.take(time_table, time_ids, axis=0, mode="clip").astype(WIDE)
        + jnp.take(class_table, class_ids, axis=0, mode="clip").astype(WIDE)
    )
    silu_cond = jax.nn.silu(condition).astype(NARROW)
    mod_local = jnp.einsum(
        "gd,dke->gke", silu_cond, ada_weight, preferred_element_type=WIDE
    ) + ada_bias.astype(WIDE)
    gathered = gather_small(mod_local.reshape(images * 6, local_width), tensor_count)
    modulation = gathered.reshape(tensor_count, images, 6, local_width).transpose(1, 2, 0, 3)
    modulation = modulation.reshape(images, 6, width)

    unit = jnp.minimum(counts[0], 1).astype(WIDE)
    arrived = lambda pairs: [tuple(part * unit for part in pair) for pair in pairs]
    attn_foreign = arrived(gather_foreign(attn_halves, tensor_count, dp_count, pieces > 1))
    mlp_foreign = arrived(gather_foreign(mlp_halves, tensor_count, dp_count, pieces > 1))

    own_qkv = qkv_weight.transpose(1, 2, 0)
    query_rows = [own_qkv[0]] + [top[:row_piece].astype(NARROW) for top, _ in attn_foreign]
    key_rows = [own_qkv[1]] + [top[row_piece : 2 * row_piece].astype(NARROW) for top, _ in attn_foreign]
    value_rows = [own_qkv[2]] + [bottom[:row_piece].astype(NARROW) for _, bottom in attn_foreign]
    proj_rows = [proj_weight] + [bottom[row_piece:].astype(NARROW) for _, bottom in attn_foreign]
    qkv_all = jnp.stack([jnp.concatenate(rows, 0) for rows in (query_rows, key_rows, value_rows)])
    proj_all = jnp.concatenate(proj_rows, 0)
    query_bias = jnp.concatenate(
        [qv_bias[0].astype(WIDE)] + [top[2 * row_piece, :row_piece] for top, _ in attn_foreign]
    )
    value_bias = jnp.concatenate(
        [qv_bias[1].astype(WIDE)]
        + [top[2 * row_piece, row_piece : 2 * row_piece] for top, _ in attn_foreign]
    )
    up_all = jnp.concatenate(
        [up_weight.transpose(1, 0)] + [top[:hidden_piece].astype(NARROW) for top, _ in mlp_foreign], 0
    )
    up_bias_all = jnp.concatenate(
        [up_bias.astype(WIDE)] + [top[hidden_piece, :hidden_piece] for top, _ in mlp_foreign]
    )
    down_all = jnp.concatenate(
        [down_weight] + [bottom.astype(NARROW) for _, bottom in mlp_foreign], 0
    )

    shift_attn = modulation[:, 0, None, :]
    scale_attn = modulation[:, 1, None, :]
    input_wide = inputs.astype(WIDE)
    normed_attn, inverse_attn = norm_parts(input_wide)
    hidden_attn = (normed_attn * (1.0 + scale_attn) + shift_attn).astype(NARROW)
    projected = jnp.einsum("gsd,ked->kgse", hidden_attn, qkv_all, preferred_element_type=WIDE)
    shape_heads = (images, length, heads, HEAD_DIM)
    query_heads = (projected[0] + query_bias).astype(NARROW).reshape(shape_heads)
    key_heads = projected[1].astype(NARROW).reshape(shape_heads)
    value_heads = (projected[2] + value_bias).astype(NARROW).reshape(shape_heads)
    scores = (
        jnp.einsum("gqhe,gkhe->ghqk", query_heads, key_heads, preferred_element_type=WIDE) * scaling
    )
    highest = jnp.max(scores, axis=-1, keepdims=True)
    exponent = jnp.exp(scores - highest)
    denominator = jnp.sum(exponent, axis=-1, keepdims=True)
    soft_probs = (exponent / denominator).astype(NARROW)
    log_total = highest + jnp.log(denominator)
    heads_out = jnp.einsum("ghqk,gkhe->gqhe", soft_probs, value_heads, preferred_element_type=WIDE)
    heads_out = heads_out.reshape(images, length, width).astype(NARROW)
    attention = jnp.einsum(
        "gse,ed->gsd", heads_out, proj_all, preferred_element_type=WIDE
    ) + proj_bias.astype(WIDE)
    (
        outputs,
        d_middle,
        d_attention,
        hidden_mlp,
        d_branch,
        activated_own,
        d_pre_own,
        sums,
    ) = mlp_pass(
        counts,
        inputs,
        attention,
        cotangent,
        modulation,
        up_all,
        up_bias_all.reshape(tensor_count, local_hidden),
        down_all,
        down_bias.astype(WIDE)[None, :],
        local_hidden,
    )
    d_gate_attn, d_shift_mlp, d_scale_mlp, d_gate_mlp = (sums[:, k] for k in range(4))
    grad_down_bias = jnp.sum(sums[:, 4], axis=0)
    grad_proj_bias = jnp.sum(sums[:, 5], axis=0)
    grad_up_bias = jnp.sum(sums[:, 6, :local_hidden], axis=0)
    grad_down_weight = jnp.einsum(
        "gsf,gsd->fd", activated_own, d_branch, preferred_element_type=WIDE
    )
    grad_up_weight = jnp.einsum("gsd,gsf->df", hidden_mlp, d_pre_own, preferred_element_type=WIDE)
    grad_proj_weight = jnp.einsum(
        "gse,gsd->ed", heads_out[:, :, :local_width], d_attention, preferred_element_type=WIDE
    )
    d_heads = jnp.einsum("gsd,ed->gse", d_attention, proj_all, preferred_element_type=WIDE)
    d_heads = d_heads.astype(NARROW).reshape(shape_heads)
    scores_again = (
        jnp.einsum("gqhe,gkhe->ghqk", query_heads, key_heads, preferred_element_type=WIDE) * scaling
    )
    probs_again = jnp.exp(scores_again - log_total)
    d_value = jnp.einsum(
        "ghqk,gqhe->gkhe", probs_again.astype(NARROW), d_heads, preferred_element_type=WIDE
    ).astype(NARROW)
    d_probs = jnp.einsum("gqhe,gkhe->ghqk", d_heads, value_heads, preferred_element_type=WIDE)
    row_inner = jnp.sum(probs_again * d_probs, axis=-1, keepdims=True)
    d_scores = (probs_again * (d_probs - row_inner)).astype(NARROW)
    d_query = (
        jnp.einsum("ghqk,gkhe->gqhe", d_scores, key_heads, preferred_element_type=WIDE) * scaling
    ).astype(NARROW)
    d_key = (
        jnp.einsum("ghqk,gqhe->gkhe", d_scores, query_heads, preferred_element_type=WIDE) * scaling
    ).astype(NARROW)
    d_projected = jnp.stack([d_query, d_key, d_value], axis=0).reshape(3, images, length, width)
    d_own = d_projected[:, :, :, :local_width]
    grad_qv_bias = jnp.stack(
        [jnp.sum(d_own[0], axis=(0, 1), dtype=WIDE), jnp.sum(d_own[2], axis=(0, 1), dtype=WIDE)]
    )
    grad_qkv_weight = jnp.einsum("gsd,kgse->dke", hidden_attn, d_own, preferred_element_type=WIDE)
    d_hidden_attn = jnp.einsum("kgse,ked->gsd", d_projected, qkv_all, preferred_element_type=WIDE)
    d_shift_attn = jnp.sum(d_hidden_attn, axis=1)
    d_scale_attn = jnp.sum(d_hidden_attn * normed_attn, axis=1)
    grad_inputs = (
        d_middle + norm_back(d_hidden_attn * (1.0 + scale_attn), normed_attn, inverse_attn)
    ).astype(NARROW)

    d_modulation = jnp.stack(
        [d_shift_attn, d_scale_attn, d_gate_attn, d_shift_mlp, d_scale_mlp, d_gate_mlp], axis=1
    )
    start_column = lax.axis_index("tensor") * local_width
    d_mod_local = lax.dynamic_slice_in_dim(d_modulation, start_column, local_width, 2)
    everyone = lambda array: lax.all_gather(array, "dp", axis=0, tiled=True)
    condition_all = everyone(condition)
    time_all = everyone(time_ids)
    class_all = everyone(class_ids)
    d_mod_all = (everyone(d_mod_local) * unit).astype(NARROW)
    silu_all = jax.nn.silu(condition_all).astype(NARROW)
    grad_ada_weight = jnp.einsum("gd,gke->dke", silu_all, d_mod_all, preferred_element_type=WIDE)
    grad_ada_bias = jnp.sum(d_mod_all, axis=0, dtype=WIDE)
    d_condition = lax.psum(
        jnp.einsum("gke,dke->gd", d_mod_all, ada_weight, preferred_element_type=WIDE), "tensor"
    )
    sigmoid_cond = jax.nn.sigmoid(condition_all)
    d_condition = d_condition * sigmoid_cond * (1.0 + condition_all * (1.0 - sigmoid_cond))
    time_pick = (time_all[None, :] == jnp.arange(time_table.shape[0], dtype=jnp.int32)[:, None])
    class_pick = (class_all[None, :] == jnp.arange(class_table.shape[0], dtype=jnp.int32)[:, None])
    exact = lax.Precision.HIGHEST
    grad_time_table = jnp.dot(time_pick.astype(WIDE), d_condition, precision=exact)
    grad_class_table = jnp.dot(class_pick.astype(WIDE), d_condition, precision=exact)

    grad_down_weight, grad_up_weight = lax.psum((grad_down_weight, grad_up_weight), "dp")
    grad_qkv_weight, grad_proj_weight = lax.psum((grad_qkv_weight, grad_proj_weight), "dp")
    grad_down_bias, grad_up_bias, grad_qv_bias, grad_proj_bias = lax.psum(
        (grad_down_bias, grad_up_bias, grad_qv_bias, grad_proj_bias), "dp"
    )
    return (
        outputs,
        grad_inputs,
        grad_time_table,
        grad_class_table,
        grad_ada_weight,
        grad_ada_bias,
        grad_qkv_weight,
        grad_qv_bias,
        grad_proj_weight,
        grad_proj_bias,
        grad_up_weight,
        grad_up_bias,
        grad_down_weight,
        grad_down_bias,
    )


def solution(mesh):
    in_specs = (
        P("dp", None, None),
        P("dp", None, None),
        P("dp"),
        P("dp"),
        P("dp"),
        P(),
        P(),
        P(None, None, "tensor"),
        P(None, "tensor"),
        P(None, None, "tensor"),
        P(None, "tensor"),
        P("tensor", None),
        P(),
        P(None, "tensor"),
        P("tensor"),
        P("tensor", None),
        P(),
    )
    out_specs = (
        P("dp", None, None),
        P("dp", None, None),
        P(),
        P(),
        P(None, None, "tensor"),
        P(None, "tensor"),
        P(None, None, "tensor"),
        P(None, "tensor"),
        P("tensor", None),
        P(),
        P(None, "tensor"),
        P("tensor"),
        P("tensor", None),
        P(),
    )

    def body(*arrays):
        return local(*arrays, tensor_count=mesh.shape["tensor"], dp_count=mesh.shape["dp"])

    return jax.shard_map(body, mesh=mesh, in_specs=in_specs, out_specs=out_specs, check_vma=False)
```
